32 devices in a mesh: graph: 8 (over y, x, core), dp: 4 (over z).
Axes of the slice: x: 2, y: 2, z: 4, core: 2. Of those that a mesh axis runs over, the one named last changes fastest.
Arguments:
- grid_latent: bfloat16 [4, 4096, 512], P('dp', 'graph'), may hold values from -6 to 6
- mesh_embed: bfloat16 [2048, 512], P('graph'), may hold values from -6 to 6
- mesh_edges: bfloat16 [12288, 512], P('graph'), may hold values from -6 to 6
- edge_geometry: bfloat16 [8, 4, 512], P('graph'), may hold values from -6 to 6
- edge_counts: int32 [8, 8], P('graph'), may hold values from 0 to 64, as said below
- edge_sources: int32 [8, 512], P('graph'), may hold values from 0 to 511
- edge_targets: int32 [8, 512], P('graph'), may hold values from 0 to 255
- halo_sources: int32 [8, 32], P('graph'), may hold values from 0 to 255
- mesh_sources: int32 [8, 1536], P('graph'), may hold values from 0 to 287, as said below
- mesh_targets: int32 [8, 1536], P('graph'), may hold values from 0 to 255
- grid_weight: bfloat16 [512, 512], replicated, may hold values from -0.25 to 0.25
- geometry_weight: float32 [4, 512], replicated, may hold values from -3 to 3
- message_weight: bfloat16 [512, 512], replicated, may hold values from -0.25 to 0.25
- mesh_update: bfloat16 [1024, 512], replicated, may hold values from -0.1875 to 0.1875
- mesh_output: bfloat16 [512, 512], replicated, may hold values from -0.25 to 0.25
- processor: bfloat16 [2, 3584, 512], replicated, may hold values from -0.15625 to 0.15625
- cotangent: bfloat16 [4, 2048, 512], P('dp', 'graph'), may hold values from -6 to 6
Outputs:
- mesh_result: bfloat16 [4, 2048, 512], P('dp', 'graph')
- mesh_gradient: bfloat16 [4, 2048, 512], P('dp', 'graph')
- gradients: bfloat16 [2, 3584, 512], replicated
The draws below stay inside these ranges and needn't reach their ends.
Inputs may be any that keep to these rules, and one draw needn't show every extreme that they name: Slots of device s for device d beyond edge_counts[s, d] are empty; every device fills all 64 slots for itself, and every device fills all 64 slots for one common device. `edge_sources`: row s holds local grid rows of device s. `edge_targets`: row d holds local mesh rows of device d, for slot c from device s at column s * 64 + c. `halo_sources`: row s, columns d * 4 to d * 4 + 3 are the local rows that device s sends to device d; every device sends 4 rows to every device, itself included. `mesh_sources`: A value under 256 is a local row; a value 256 + s * 4 + k is halo slot k from device s.
All inputs are finite; a program needn't handle non-finite values.
Results may differ from the reference program's by a relative error of at most 0.024.
Values may be sent and summed in bfloat16 or wider, within the bound.
No kernel may reach another device: no remote copies, remote signals or barrier semaphores. Data moves between devices by JAX's collectives and lax.ppermute only.
A program may use at most 128 MiB of HBM per device.

```python
import math
import jax
import jax.numpy as jnp
from jax import lax

D = 512
GD = 512
MD = 256
EMD = 1536
CAP = 64
HB = 4
L = 2
SAMPLES = 4
GRID = 4096
MESH = 2048
EDGES = 12288
N_GRAPH = 8
N_DP = 4


def draw_edge_counts(key, part):
    nearby_key, distant_key, hottest_key = jax.random.split(jax.random.fold_in(key, 11), 3)
    peers = N_GRAPH
    nearby_counts = jax.random.randint(nearby_key, (peers, peers), CAP // 2, CAP + 1)
    distant_counts = jax.random.randint(distant_key, (peers, peers), CAP // 4, CAP // 2 + 1)
    source = jnp.arange(peers, dtype=jnp.int32)[:, None]
    target = jnp.arange(peers, dtype=jnp.int32)[None, :]
    offset = (target - source) % peers
    nearby = (offset == 1) | (offset == 2) | (offset == peers - 1)
    counts = jnp.where(nearby, nearby_counts, distant_counts)
    hottest = jax.random.randint(hottest_key, (), 0, peers)
    counts = jnp.where((offset == 0) | (target == hottest), CAP, counts)
    return counts.astype(jnp.int32)


def draw_mesh_sources(key, part):
    local_key, remote_key, choose_key = jax.random.split(jax.random.fold_in(key, 23), 3)
    extent = (N_GRAPH, EMD)
    local_rows = jax.random.randint(local_key, extent, 0, MD)
    remote_rows = jax.random.randint(remote_key, extent, MD, MD + N_GRAPH * HB)
    remote = jax.random.randint(choose_key, extent, 0, 4) == 0
    return jnp.where(remote, remote_rows, local_rows).astype(jnp.int32)


def with_ends(values, stream_key, smallest, high):
    shape = values.shape
    place = [jax.random.randint(jax.random.fold_in(stream_key, axis), (), 0, shape[axis]) for axis in range(len(shape))]
    values = values.at[tuple(place)].set(smallest)
    longest = shape.index(max(shape))
    place[longest] = (place[longest] + 1) % shape[longest]
    return values.at[tuple(place)].set(high)


def level_of(own_key, shape, cuts, low, largest):
    loudness, own = 1.0, jax.random.fold_in(own_key, 6)
    for axis_at, parts in cuts:
        draws = jnp.exp(jax.random.uniform(jax.random.fold_in(own, axis_at), (parts,), jnp.float32, low / len(cuts), largest / len(cuts)))
        loudness = loudness * jnp.repeat(draws, shape[axis_at] // parts).reshape([-1 if axis == axis_at else 1 for axis in range(len(shape))])
    return loudness


def noise(rng, shape, spread, limit, cuts=(), held_as=jnp.bfloat16):
    entries = jax.random.normal(rng, shape, jnp.float32) * spread
    if len(cuts) > 0:
        entries = level_of(rng, shape, cuts, -0.22, 0.18) * entries
    return jnp.clip(entries, min=-limit, max=limit).astype(held_as)


def setup_inputs(seed: int = 0) -> dict:
    key_of = jax.random.split(jax.random.key(seed), 18)
    grid_latent = noise(key_of[0], (SAMPLES, GRID, D), 1.0, 6.0, ((0, 4), (1, 8)))
    mesh_embed = noise(key_of[1], (MESH, D), 1.0, 6.0, ((0, 8),))
    mesh_edges = noise(key_of[2], (EDGES, D), 1.0, 6.0, ((0, 8),))
    edge_geometry = noise(key_of[3], (N_GRAPH, 4, N_GRAPH * CAP), 1.0, 6.0, ((0, 8),))
    edge_counts = draw_edge_counts(jax.random.fold_in(key_of[17], 71), 0)
    edge_sources = with_ends(jax.random.randint(key_of[5], (N_GRAPH, N_GRAPH * CAP), 0, GD), jax.random.fold_in(key_of[5], 1), 0, GD - 1).astype(jnp.int32)
    edge_targets = with_ends(jax.random.randint(key_of[6], (N_GRAPH, N_GRAPH * CAP), 0, MD), jax.random.fold_in(key_of[6], 1), 0, MD - 1).astype(jnp.int32)
    halo_sources = with_ends(jax.random.randint(key_of[7], (N_GRAPH, N_GRAPH * HB), 0, MD), jax.random.fold_in(key_of[7], 1), 0, MD - 1).astype(jnp.int32)
    mesh_sources = draw_mesh_sources(jax.random.fold_in(key_of[17], 71), 0)
    mesh_targets = with_ends(jax.random.randint(key_of[9], (N_GRAPH, EMD), 0, MD), jax.random.fold_in(key_of[9], 1), 0, MD - 1).astype(jnp.int32)
    grid_weight = noise(key_of[10], (D, D), D ** -0.5, 0.25)
    geometry_weight = noise(key_of[11], (4, D), 4 ** -0.5, 3.0, (), jnp.float32)
    message_weight = noise(key_of[12], (D, D), D ** -0.5, 0.25)
    mesh_update = noise(key_of[13], (2 * D, D), (2 * D) ** -0.5, 0.1875)
    mesh_output = noise(key_of[14], (D, D), D ** -0.5, 0.25)
    processor = noise(key_of[15], (L, 7 * D, D), (3 * D) ** -0.5, 0.15625)
    cotangent = noise(key_of[16], (SAMPLES, MESH, D), 1.0, 6.0, ((0, 4), (1, 8)))
    return {"grid_latent": grid_latent, "mesh_embed": mesh_embed, "mesh_edges": mesh_edges, "edge_geometry": edge_geometry, "edge_counts": edge_counts, "edge_sources": edge_sources, "edge_targets": edge_targets, "halo_sources": halo_sources, "mesh_sources": mesh_sources, "mesh_targets": mesh_targets, "grid_weight": grid_weight, "geometry_weight": geometry_weight, "message_weight": message_weight, "mesh_update": mesh_update, "mesh_output": mesh_output, "processor": processor, "cotangent": cotangent}


EPSILON = 1e-05
HIGHEST = lax.Precision.HIGHEST

def matmul(left, right):
    return jnp.dot(left, right, preferred_element_type=jnp.float32)

def weight_grad(left, right):
    return lax.dot_general(left, right, (((0,), (0,)), ((), ())), preferred_element_type=jnp.float32)

def input_grad(left, right):
    return lax.dot_general(left, right, (((1,), (1,)), ((), ())), preferred_element_type=jnp.float32)

def normalize(values):
    center = lax.optimization_barrier(jnp.mean(values, axis=-1, keepdims=True))
    shifted = values - center
    inverse = lax.rsqrt(lax.optimization_barrier(jnp.mean(shifted * shifted, axis=-1, keepdims=True)) + EPSILON)
    return (shifted * inverse, inverse)

def normalize_back(normed, inverse, upstream):
    first_mean = lax.optimization_barrier(jnp.mean(upstream, axis=-1, keepdims=True))
    second_mean = lax.optimization_barrier(jnp.mean(upstream * normed, axis=-1, keepdims=True))
    return inverse * (upstream - first_mean - normed * second_mean)

def swish_slope(values):
    sigma = jax.nn.sigmoid(values)
    return sigma * (1.0 + values * (1.0 - sigma))

def encode(grid_rows, mesh_embed, edge_geometry, edge_counts, edge_sources, edge_targets, grid_weight, geometry_weight, message_weight, mesh_update, mesh_output):
    width = mesh_embed.shape[1]
    peers = edge_counts.shape[0]
    slots = edge_sources.shape[1]
    capacity = slots // peers
    device = jnp.arange(peers).astype(jnp.int32)[:, None]
    position = jnp.arange(slots).astype(jnp.int32)[None, :]
    target_peer = position // capacity
    column = position % capacity
    senders = (device * GD + edge_sources).reshape(-1)
    targets = (target_peer * MD + edge_targets[target_peer, device * capacity + column]).reshape(-1)
    live = (column < edge_counts[device, target_peer]).reshape(-1)
    geometry = jnp.transpose(edge_geometry.astype(jnp.float32), (1, 0, 2)).reshape(4, -1)
    geometry_term = jnp.einsum('fs,fd->sd', geometry, geometry_weight, precision=HIGHEST)
    grid_proj = matmul(grid_rows, grid_weight)
    messages = jnp.where(live[:, None], jax.nn.silu(grid_proj[senders] + geometry_term), 0.0).astype(jnp.bfloat16)
    hidden_sum = jax.ops.segment_sum(messages.astype(jnp.float32), targets, num_segments=MESH).astype(jnp.bfloat16)
    aggregate = matmul(hidden_sum, message_weight).astype(jnp.bfloat16)
    pre_update = matmul(mesh_embed, mesh_update[:width]) + matmul(aggregate, mesh_update[width:])
    normed, inverse = normalize(matmul(jax.nn.silu(pre_update).astype(jnp.bfloat16), mesh_output))
    return (mesh_embed.astype(jnp.float32) + normed).astype(jnp.bfloat16)

def mesh_indices(halo_sources, mesh_sources, mesh_targets):
    peers = mesh_sources.shape[0]
    device = jnp.arange(peers).astype(jnp.int32)[:, None]
    local = mesh_sources < MD
    halo_slot = jnp.maximum(mesh_sources - MD, 0)
    source = halo_slot // HB
    within = halo_slot % HB
    remote_rows = halo_sources[source, device * HB + within]
    senders = jnp.where(local, device * MD + mesh_sources, source * MD + remote_rows).reshape(-1)
    receivers = (device * MD + mesh_targets).reshape(-1)
    return (senders.astype(jnp.int32), receivers.astype(jnp.int32))

def layer_forward(nodes, edges, senders, receivers, weights):
    width = nodes.shape[1]
    send_proj = matmul(nodes, weights[width:2 * width])
    recv_proj = matmul(nodes, weights[2 * width:3 * width])
    pre_edge = matmul(edges, weights[:width]) + send_proj[senders] + recv_proj[receivers]
    hidden_edge = jax.nn.silu(pre_edge).astype(jnp.bfloat16)
    normed_edge, inverse_edge = normalize(matmul(hidden_edge, weights[3 * width:4 * width]))
    new_edges = (edges.astype(jnp.float32) + normed_edge).astype(jnp.bfloat16)
    summed = jax.ops.segment_sum(new_edges.astype(jnp.float32), receivers, num_segments=MESH).astype(jnp.bfloat16)
    pre_node = matmul(nodes, weights[4 * width:5 * width]) + matmul(summed, weights[5 * width:6 * width])
    hidden_node = jax.nn.silu(pre_node).astype(jnp.bfloat16)
    normed_node, inverse_node = normalize(matmul(hidden_node, weights[6 * width:]))
    new_nodes = (nodes.astype(jnp.float32) + normed_node).astype(jnp.bfloat16)
    saved = (pre_edge, hidden_edge, normed_edge, inverse_edge, summed, pre_node, hidden_node, normed_node, inverse_node)
    return (new_nodes, new_edges, saved)

def layer_backward(nodes, edges, senders, receivers, weights, saved, grad_nodes, grad_edges):
    width = nodes.shape[1]
    pre_edge, hidden_edge, normed_edge, inverse_edge, summed, pre_node, hidden_node, normed_node, inverse_node = saved
    q_node = normalize_back(normed_node, inverse_node, grad_nodes).astype(jnp.bfloat16)
    grad_node_second = weight_grad(hidden_node, q_node)
    d_node = (input_grad(q_node, weights[6 * width:]) * swish_slope(pre_node)).astype(jnp.bfloat16)
    grad_node_own = weight_grad(nodes, d_node)
    grad_node_sum = weight_grad(summed, d_node)
    grad_summed = input_grad(d_node, weights[5 * width:6 * width])
    edge_upstream = grad_edges + grad_summed[receivers]
    q_edge = normalize_back(normed_edge, inverse_edge, edge_upstream).astype(jnp.bfloat16)
    grad_edge_second = weight_grad(hidden_edge, q_edge)
    d_edge = input_grad(q_edge, weights[3 * width:4 * width]) * swish_slope(pre_edge)
    d_edge16 = d_edge.astype(jnp.bfloat16)
    grad_send = jax.ops.segment_sum(d_edge, senders, num_segments=MESH).astype(jnp.bfloat16)
    grad_recv = jax.ops.segment_sum(d_edge, receivers, num_segments=MESH).astype(jnp.bfloat16)
    partial_value = jnp.concatenate([weight_grad(edges, d_edge16), weight_grad(nodes, grad_send), weight_grad(nodes, grad_recv), grad_edge_second, grad_node_own, grad_node_sum, grad_node_second], 0)
    new_grad_edges = edge_upstream + input_grad(d_edge16, weights[:width])
    new_grad_nodes = grad_nodes + input_grad(d_node, weights[4 * width:5 * width]) + input_grad(grad_send, weights[width:2 * width]) + input_grad(grad_recv, weights[2 * width:3 * width])
    return (new_grad_nodes, new_grad_edges, partial_value)

def reference(grid_latent, mesh_embed, mesh_edges, edge_geometry, edge_counts, edge_sources, edge_targets, halo_sources, mesh_sources, mesh_targets, grid_weight, geometry_weight, message_weight, mesh_update, mesh_output, processor, cotangent):
    senders, receivers = mesh_indices(halo_sources, mesh_sources, mesh_targets)
    layers = processor.shape[0]
    scale = 1.0 / math.sqrt(N_DP * MESH)

    def one_sample(inputs):
        grid_rows, upstream = inputs
        nodes = encode(grid_rows, mesh_embed, edge_geometry, edge_counts, edge_sources, edge_targets, grid_weight, geometry_weight, message_weight, mesh_update, mesh_output)
        edges = mesh_edges
        stored = []
        for layer_index in range(layers):
            new_nodes, new_edges, saved = layer_forward(nodes, edges, senders, receivers, processor[layer_index])
            stored.append((nodes, edges, saved))
            nodes, edges = (new_nodes, new_edges)
        result = nodes
        grad_nodes = upstream.astype(jnp.float32)
        grad_edges = jnp.zeros(edges.shape, jnp.float32)
        pieces = [None] * layers
        for layer_index in reversed(range(layers)):
            layer_nodes, layer_edges, saved = stored[layer_index]
            grad_nodes, grad_edges, partial_value = layer_backward(layer_nodes, layer_edges, senders, receivers, processor[layer_index], saved, grad_nodes, grad_edges)
            pieces[layer_index] = partial_value * scale
        return (result, grad_nodes.astype(jnp.bfloat16), jnp.stack(pieces))
    results, node_grads, partials = lax.map(one_sample, (grid_latent, cotangent))
    gradients = lax.optimization_barrier(jnp.sum(partials, axis=0)).astype(jnp.bfloat16)
    return (results, node_grads, gradients)
```

```python
import functools
import math

import jax
import jax.numpy as jnp
from jax import lax
from jax.experimental import pallas as pl
from jax.experimental.pallas import tpu as pltpu
from jax.sharding import PartitionSpec as P

EPSILON = 1e-05
F32 = jnp.float32
BF16 = jnp.bfloat16
BLOCK = 256
VMEM_LIMIT = 60 * 1024 * 1024


def mm(left, right):
    return jnp.dot(left, right, preferred_element_type=F32)


def mm_t(left, right):
    return lax.dot_general(left, right, (((0,), (0,)), ((), ())), preferred_element_type=F32)


def mm_bt(left, right):
    return lax.dot_general(left, right, (((1,), (1,)), ((), ())), preferred_element_type=F32)


def sigmoid(values):
    return 0.5 + 0.5 * jnp.tanh(0.5 * values)


def silu(values):
    return values * sigmoid(values)


def slope(values):
    sigma = sigmoid(values)
    return sigma * (1.0 + values * (1.0 - sigma))


def normalize(values):
    center = jnp.mean(values, axis=-1, keepdims=True)
    shifted = values - center
    inverse = lax.rsqrt(jnp.mean(shifted * shifted, axis=-1, keepdims=True) + EPSILON)
    return shifted * inverse, inverse


def normalize_back(normed, inverse, upstream):
    first = jnp.mean(upstream, axis=-1, keepdims=True)
    second = jnp.mean(upstream * normed, axis=-1, keepdims=True)
    return inverse * (upstream - first - normed * second)


def one_hot(row, count):
    rows = lax.broadcasted_iota(jnp.int32, (count, row.shape[1]), 0)
    return (rows == row).astype(BF16)


def row_block(array, width, at, block):
    return array[at * width : (at + block) * width, :]


def message_kernel(grid_ref, weight_ref, geometry_ref, geometry_weight_ref, counts_ref, sources_ref, out_ref):
    slots = sources_ref.shape[1]
    peers = counts_ref.shape[1]
    capacity = slots // peers
    position = lax.broadcasted_iota(jnp.int32, (1, slots), 1)
    live = jnp.zeros((1, slots), jnp.int32)
    for peer in range(peers):
        start = peer * capacity
        inside = (position >= start) & (position < start + counts_ref[0, peer]) & (position < start + capacity)
        live = jnp.where(inside, 1, live)
    sources = jnp.where(live > 0, sources_ref[...], -1)
    geometry = jnp.where(live > 0, geometry_ref[0].astype(F32), 0.0).astype(BF16)
    weight = geometry_weight_ref[...]
    high = weight.astype(BF16)
    rest = weight - high.astype(F32)
    middle = rest.astype(BF16)
    low = (rest - middle.astype(F32)).astype(BF16)
    left = jnp.concatenate([geometry] * 3, 0)
    right = jnp.concatenate([high, middle, low], 0)
    rows = mm_t(one_hot(sources, grid_ref.shape[1]), grid_ref[0]).astype(BF16)
    out_ref[...] = silu(mm(rows, weight_ref[...]) + mm_t(left, right)).astype(BF16)


def start_kernel(arrived_ref, targets_ref, embed_ref, message_ref, update_ref, output_ref, halo_ref, nodes_ref, send_ref):
    count, width = embed_ref.shape
    hidden = mm(one_hot(targets_ref[...], count), arrived_ref[...]).astype(BF16)
    aggregate = mm(hidden, message_ref[...]).astype(BF16)
    embed = embed_ref[...]
    pre = mm(embed, update_ref[:width, :]) + mm(aggregate, update_ref[width:, :])
    normed, _ = normalize(mm(silu(pre).astype(BF16), output_ref[...]))
    nodes = (embed.astype(F32) + normed).astype(BF16)
    nodes_ref[...] = nodes
    send_ref[...] = mm_t(one_hot(halo_ref[...], count), nodes).astype(BF16)


def build_tables(senders_ref, receivers_ref, table_ref, count, extended):
    table_ref[:extended, :] = one_hot(senders_ref[...], extended)
    table_ref[extended:, :] = one_hot(receivers_ref[...], count)


def layer_forward(
    nodes_ref, halo_rows_ref, edges_ref, weights_ref, table_ref, projected_ref,
    pre_ref, hidden_ref, normed_ref, inverse_ref, new_edges_ref,
):
    count, width = nodes_ref.shape
    extended = count + halo_rows_ref.shape[0]
    nodes = nodes_ref[...]
    ws = weights_ref[width : 2 * width, :]
    projected_ref[:count, :] = mm(nodes, ws).astype(BF16)
    projected_ref[count:extended, :] = mm(halo_rows_ref[...], ws).astype(BF16)
    projected_ref[extended:, :] = mm(nodes, weights_ref[2 * width : 3 * width, :]).astype(BF16)

    def body(step, carry):
        rows = pl.ds(pl.multiple_of(step * BLOCK, BLOCK), BLOCK)
        edges = edges_ref[rows, :]
        pre = mm(edges, weights_ref[:width, :]) + mm_t(table_ref[:, rows], projected_ref[...])
        pre_ref[rows, :] = pre.astype(pre_ref.dtype)
        hidden = silu(pre).astype(BF16)
        hidden_ref[rows, :] = hidden
        normed, inverse = normalize(mm(hidden, weights_ref[3 * width : 4 * width, :]))
        normed_ref[rows, :] = normed.astype(normed_ref.dtype)
        inverse_ref[rows, :] = inverse
        new_edges_ref[rows, :] = (edges.astype(F32) + normed).astype(BF16)
        return carry

    lax.fori_loop(0, edges_ref.shape[0] // BLOCK, body, 0)
    summed = mm(table_ref[extended:, :], new_edges_ref[...]).astype(BF16)
    pre_node = mm(nodes, weights_ref[4 * width : 5 * width, :]) + mm(summed, weights_ref[5 * width : 6 * width, :])
    hidden_node = silu(pre_node).astype(BF16)
    normed_node, inverse_node = normalize(mm(hidden_node, weights_ref[6 * width :, :]))
    new_nodes = (nodes.astype(F32) + normed_node).astype(BF16)
    return summed, pre_node, hidden_node, normed_node, inverse_node, new_nodes


def layer_backward(
    scale, grad, summed, pre_node, hidden_node, normed_node, inverse_node,
    nodes_ref, halo_rows_ref, edges_ref, weights_ref, table_ref,
    pre_ref, hidden_ref, normed_ref, inverse_ref, grad_edges_in_ref,
    q_ref, d_ref, pieces_ref, grad_edges_out_ref, sums_ref, halo_out_ref, grad_ref,
):
    count, width = nodes_ref.shape
    extended = count + halo_rows_ref.shape[0]
    nodes = nodes_ref[...]

    def put(at, value):
        pieces_ref[at * width : (at + 1) * width, :] = (value * scale).astype(BF16)

    q_node = normalize_back(normed_node, inverse_node, grad).astype(BF16)
    put(6, mm_t(hidden_node, q_node))
    d_node = (mm_bt(q_node, weights_ref[6 * width :, :]) * slope(pre_node)).astype(BF16)
    put(4, mm_t(nodes, d_node))
    put(5, mm_t(summed, d_node))
    grad_summed = mm_bt(d_node, weights_ref[5 * width : 6 * width, :]).astype(BF16)

    def body(step, carry):
        rows = pl.ds(pl.multiple_of(step * BLOCK, BLOCK), BLOCK)
        upstream = mm_t(table_ref[extended:, rows], grad_summed)
        if grad_edges_in_ref is not None:
            upstream = upstream + grad_edges_in_ref[rows, :].astype(F32)
        q_edge = normalize_back(normed_ref[rows, :].astype(F32), inverse_ref[rows, :], upstream).astype(BF16)
        q_ref[rows, :] = q_edge
        d_edge = mm_bt(q_edge, weights_ref[3 * width : 4 * width, :]) * slope(pre_ref[rows, :].astype(F32))
        d_edge = d_edge.astype(BF16)
        d_ref[rows, :] = d_edge
        if grad_edges_out_ref is not None:
            grad_edges_out_ref[rows, :] = (upstream + mm_bt(d_edge, weights_ref[:width, :])).astype(BF16)
        return carry

    lax.fori_loop(0, edges_ref.shape[0] // BLOCK, body, 0)
    put(0, mm_t(edges_ref[...], d_ref[...]))
    put(3, mm_t(hidden_ref[...], q_ref[...]))
    sums = mm(table_ref[...], d_ref[...])
    sent = sums[:extended]
    received = sums[extended:].astype(BF16)
    sent16 = sent.astype(BF16)
    put(1, mm_t(nodes, sent16[:count]) + mm_t(halo_rows_ref[...], sent16[count:]))
    put(2, mm_t(nodes, received))
    sums_ref[...] = sent[:count]
    halo_out_ref[...] = sent16[count:]
    grad_ref[...] = (
        grad
        + mm_bt(d_node, weights_ref[4 * width : 5 * width, :])
        + mm_bt(received, weights_ref[2 * width : 3 * width, :])
    )


def complete_gradient(partial_ref, sums_ref, returned_ref, halo_ref, weight):
    count = partial_ref.shape[0]
    total = sums_ref[...] + mm(one_hot(halo_ref[...], count), returned_ref[...])
    return partial_ref[...] + mm_bt(total.astype(BF16), weight)


def forward_kernel(
    nodes_ref, halo_rows_ref, edges_ref, weights_ref, senders_ref, receivers_ref, halo_ref,
    new_nodes_ref, send_ref, new_edges_ref, pre_ref, hidden_ref, normed_ref, inverse_ref,
    summed_ref, pre_node_ref, hidden_node_ref, normed_node_ref, inverse_node_ref,
    table_ref, projected_ref,
):
    count = nodes_ref.shape[0]
    build_tables(senders_ref, receivers_ref, table_ref, count, count + halo_rows_ref.shape[0])
    summed, pre_node, hidden_node, normed_node, inverse_node, new_nodes = layer_forward(
        nodes_ref, halo_rows_ref, edges_ref, weights_ref, table_ref, projected_ref,
        pre_ref, hidden_ref, normed_ref, inverse_ref, new_edges_ref,
    )
    summed_ref[...] = summed
    pre_node_ref[...] = pre_node
    hidden_node_ref[...] = hidden_node
    normed_node_ref[...] = normed_node
    inverse_node_ref[...] = inverse_node
    new_nodes_ref[...] = new_nodes
    send_ref[...] = mm_t(one_hot(halo_ref[...], count), new_nodes).astype(BF16)


def last_kernel(
    scale, nodes_ref, halo_rows_ref, edges_ref, weights_ref, senders_ref, receivers_ref, cotangent_ref,
    result_ref, pieces_ref, grad_edges_ref, sums_ref, halo_out_ref, grad_ref,
    table_ref, projected_ref, pre_ref, hidden_ref, normed_ref, inverse_ref, new_edges_ref, q_ref, d_ref,
):
    count = nodes_ref.shape[0]
    build_tables(senders_ref, receivers_ref, table_ref, count, count + halo_rows_ref.shape[0])
    summed, pre_node, hidden_node, normed_node, inverse_node, new_nodes = layer_forward(
        nodes_ref, halo_rows_ref, edges_ref, weights_ref, table_ref, projected_ref,
        pre_ref, hidden_ref, normed_ref, inverse_ref, new_edges_ref,
    )
    result_ref[0] = new_nodes
    layer_backward(
        scale, cotangent_ref[0].astype(F32), summed, pre_node, hidden_node, normed_node, inverse_node,
        nodes_ref, halo_rows_ref, edges_ref, weights_ref, table_ref,
        pre_ref, hidden_ref, normed_ref, inverse_ref, None,
        q_ref, d_ref, pieces_ref, grad_edges_ref, sums_ref, halo_out_ref, grad_ref,
    )


def backward_kernel(
    scale, first, nodes_ref, halo_rows_ref, edges_ref, weights_ref, senders_ref, receivers_ref, halo_ref,
    pre_ref, hidden_ref, normed_ref, inverse_ref,
    summed_ref, pre_node_ref, hidden_node_ref, normed_node_ref, inverse_node_ref,
    grad_edges_in_ref, partial_ref, later_sums_ref, returned_ref, later_weights_ref, *rest,
):
    outs, (table_ref, q_ref, d_ref) = rest[:-3], rest[-3:]
    if first:
        (pieces_ref, sums_ref, halo_out_ref, grad_ref), grad_edges_ref = outs, None
    else:
        pieces_ref, grad_edges_ref, sums_ref, halo_out_ref, grad_ref = outs
    count = nodes_ref.shape[0]
    build_tables(senders_ref, receivers_ref, table_ref, count, count + halo_rows_ref.shape[0])
    grad = complete_gradient(partial_ref, later_sums_ref, returned_ref, halo_ref, later_weights_ref[...])
    layer_backward(
        scale, grad, summed_ref[...], pre_node_ref[...], hidden_node_ref[...], normed_node_ref[...],
        inverse_node_ref[...], nodes_ref, halo_rows_ref, edges_ref, weights_ref, table_ref,
        pre_ref, hidden_ref, normed_ref, inverse_ref, grad_edges_in_ref,
        q_ref, d_ref, pieces_ref, grad_edges_ref, sums_ref, halo_out_ref, grad_ref,
    )


def finish_kernel(partial_ref, sums_ref, returned_ref, halo_ref, weights_ref, out_ref):
    out_ref[0] = complete_gradient(partial_ref, sums_ref, returned_ref, halo_ref, weights_ref[...]).astype(BF16)


def whole(array):
    rank = len(array.shape)
    return pl.BlockSpec(array.shape, lambda i: (0,) * rank, pipeline_mode=pl.Buffered(1))


def call(kernel, args, specs, outs, scratch=(), name=None):
    return pl.pallas_call(
        kernel,
        grid=(1,),
        in_specs=[whole(a) if s is None else s for a, s in zip(args, specs, strict=True)],
        out_specs=[whole(o) for o in outs],
        out_shape=outs,
        scratch_shapes=list(scratch),
        compiler_params=pltpu.CompilerParams(vmem_limit_bytes=VMEM_LIMIT),
        name=name,
    )(*args)


def shape(*dims, dtype=BF16):
    return jax.ShapeDtypeStruct(dims, dtype)


def pairs(size, bit):
    return [(at, at ^ bit) for at in range(size)]


def halve(rows, axis, bit):
    side = (lax.axis_index(axis) // bit) % 2
    halves = rows.reshape(2, rows.shape[0] // 2, rows.shape[1])
    mine = lax.dynamic_index_in_dim(halves, side, 0, keepdims=False)
    other = lax.dynamic_index_in_dim(halves, 1 - side, 0, keepdims=False)
    got = lax.ppermute(other, axis, pairs(lax.axis_size(axis), bit))
    return (got.astype(F32) + mine.astype(F32)).astype(BF16)


def double(rows, axis, bit):
    side = (lax.axis_index(axis) // bit) % 2
    got = lax.ppermute(rows, axis, pairs(lax.axis_size(axis), bit))
    return jnp.where(side == 0, jnp.concatenate([rows, got], 0), jnp.concatenate([got, rows], 0))


def split3(count, unit):
    third = -(-count // (3 * unit)) * unit
    return (third, third, count - 2 * third)


def cut(rows, sizes):
    out, at = [], 0
    for size in sizes:
        out.append(rows[at : at + size])
        at += size
    return out


def reduce_all(rows):
    graph, dp = lax.axis_size("graph"), lax.axis_size("dp")
    steps = [("graph", 1 << b) for b in range(1, graph.bit_length() - 1)]
    steps += [("dp", 1 << b) for b in range(dp.bit_length() - 1)]
    core, mixed, tail = ("graph", 1), steps[:3], steps[3:]
    orders = [mixed[k:] + mixed[:k] for k in range(3)]
    rows = halve(rows, *core)
    sizes = split3(rows.shape[0], 128)
    parts = cut(rows, sizes)
    for stage in range(3):
        parts = [halve(part, *order[stage]) for part, order in zip(parts, orders)]
    rows = jnp.concatenate(parts, 0)
    for step in tail:
        rows = halve(rows, *step)
    for step in reversed(tail):
        rows = double(rows, *step)
    parts = cut(rows, [size // 8 for size in sizes])
    for stage in (2, 1, 0):
        parts = [double(part, *order[stage]) for part, order in zip(parts, orders)]
    return double(jnp.concatenate(parts, 0), *core)


def exchange(rows):
    return lax.all_to_all(rows, "graph", split_axis=0, concat_axis=0, tiled=True)


def on_device(
    grid_latent, mesh_embed, mesh_edges, edge_geometry, edge_counts, edge_sources, edge_targets, halo_sources,
    mesh_sources, mesh_targets, grid_weight, geometry_weight, message_weight, mesh_update, mesh_output, processor,
    cotangent,
):
    count, width = mesh_embed.shape
    slots = edge_sources.shape[1]
    edge_rows = mesh_edges.shape[0]
    halo = halo_sources.shape[1]
    extended = count + halo
    layers, weight_rows = processor.shape[:2]
    scale = 1.0 / math.sqrt(lax.axis_size("dp") * lax.axis_size("graph") * count)

    def layer_weights(layer):
        return pl.BlockSpec((None, weight_rows, width), lambda i: (layer, 0, 0), pipeline_mode=pl.Buffered(1))

    def sender_weights(layer):
        return pl.BlockSpec((None, width, width), lambda i: (layer, 1, 0), pipeline_mode=pl.Buffered(1))

    (messages,) = call(
        message_kernel,
        (grid_latent, grid_weight, edge_geometry, geometry_weight, edge_counts, edge_sources),
        (None, None, None, None, pl.BlockSpec(memory_space=pltpu.SMEM), None),
        [shape(slots, width)],
        name="messages",
    )
    nodes, send = call(
        start_kernel,
        (exchange(messages), edge_targets, mesh_embed, message_weight, mesh_update, mesh_output, halo_sources),
        (None,) * 7,
        [shape(count, width), shape(halo, width)],
        name="start",
    )
    table = pltpu.VMEM((extended + count, edge_rows), BF16)
    projected = pltpu.VMEM((extended + count, width), BF16)
    edge16 = pltpu.VMEM((edge_rows, width), BF16)
    edge32 = pltpu.VMEM((edge_rows, width), F32)
    edge1 = pltpu.VMEM((edge_rows, 1), F32)
    edges = mesh_edges
    stored = []
    for layer in range(layers - 1):
        incoming = exchange(send)
        outs = call(
            forward_kernel,
            (nodes, incoming, edges, processor, mesh_sources, mesh_targets, halo_sources),
            (None, None, None, layer_weights(layer), None, None, None),
            [
                shape(count, width), shape(halo, width), shape(edge_rows, width),
                shape(edge_rows, width), shape(edge_rows, width), shape(edge_rows, width),
                shape(edge_rows, 1, dtype=F32),
                shape(count, width), shape(count, width, dtype=F32), shape(count, width),
                shape(count, width, dtype=F32), shape(count, 1, dtype=F32),
            ],
            (table, projected),
            name="forward",
        )
        stored.append((nodes, incoming, edges, outs[3:]))
        nodes, send, edges = outs[:3]
    incoming = exchange(send)
    piece = shape(weight_rows, width)
    tail = [shape(count, width, dtype=F32), shape(halo, width), shape(count, width, dtype=F32)]
    result, last_piece, grad_edges, sums, halo_out, partial = call(
        functools.partial(last_kernel, scale),
        (nodes, incoming, edges, processor, mesh_sources, mesh_targets, cotangent),
        (None, None, None, layer_weights(layers - 1), None, None, None),
        [shape(1, count, width), piece, shape(edge_rows, width), *tail],
        (table, projected, edge32, edge16, edge32, edge1, edge16, edge16, edge16),
        name="last",
    )
    pieces = [last_piece]
    for layer in reversed(range(layers - 1)):
        first = layer == 0
        layer_nodes, layer_halo, layer_edges, saved = stored[layer]
        outs = call(
            functools.partial(backward_kernel, scale, first),
            (
                layer_nodes, layer_halo, layer_edges, processor, mesh_sources, mesh_targets, halo_sources, *saved,
                grad_edges, partial, sums, exchange(halo_out), processor,
            ),
            (None, None, None, layer_weights(layer)) + (None,) * (3 + len(saved) + 4) + (sender_weights(layer + 1),),
            [piece, *tail] if first else [piece, shape(edge_rows, width), *tail],
            (table, edge16, edge16),
            name="backward",
        )
        pieces.insert(0, outs[0])
        if not first:
            grad_edges = outs[1]
        sums, halo_out, partial = outs[-3:]
    (gradient,) = call(
        finish_kernel,
        (partial, sums, exchange(halo_out), halo_sources, processor),
        (None, None, None, None, sender_weights(0)),
        [shape(1, count, width)],
        name="finish",
    )
    gradients = reduce_all(jnp.concatenate(pieces, 0)).reshape(layers, weight_rows, width)
    return result, gradient, gradients


def solution(mesh):
    in_specs = (
        P("dp", "graph", None),
        P("graph", None),
        P("graph", None),
        P("graph", None, None),
        P("graph", None),
        P("graph", None),
        P("graph", None),
        P("graph", None),
        P("graph", None),
        P("graph", None),
        P(),
        P(),
        P(),
        P(),
        P(),
        P(),
        P("dp", "graph", None),
    )
    out_specs = (P("dp", "graph", None), P("dp", "graph", None), P())
    return jax.shard_map(on_device, mesh=mesh, in_specs=in_specs, out_specs=out_specs, check_vma=False)
```
